256 devices in a mesh: ex: 8 (over z), ey: 4 (over x_hi, core), ez: 8 (over y, x_lo).
Axes of the slice: x: 4 (x_hi: 2, x_lo: 2; x = x_hi * 2 + x_lo), y: 4, z: 8, core: 2. Of those that a mesh axis runs over, the one named last changes fastest.
Arguments:
- load_raw: float32 [16, 8, 32, 32, 384], P('ex', 'ey', 'ez'), may hold values from -8 to 8
- scaling: float32 [16, 8, 32, 384], P('ex', 'ey', 'ez'), may hold values from 0.6 to 1.8
- fine_matrix: float32 [384, 384], replicated
- fine_inverse: float32 [384, 384], replicated
- prolong_four: float32 [384, 98], replicated
- coarse_four: float32 [98, 98], replicated
- prolong_two: float32 [384, 26], replicated
- coarse_two: float32 [26, 26], replicated
- orient: int32 [3, 16, 8, 32], P(None, 'ex', 'ey', 'ez'), may hold values from 0 to 3
- boundary: int32 [6, 16, 8, 32], P(None, 'ex', 'ey', 'ez'), may hold values from 0 to 1
Outputs:
- solution: float32 [16, 8, 32, 32, 384], P('ex', 'ey', 'ez')
The draws below stay inside these ranges and needn't reach their ends.
All inputs are finite; a program needn't handle non-finite values.
Results may differ from the reference program's by a relative error of at most 0.0001.
Values sent between devices are 32-bit elements; how exact they have to be, the bound alone decides.
A program may use at most 64 MiB of HBM per device.

```python
import math
import jax
import jax.numpy as jnp
from jax import lax

SPECIES = 32
FACE_SIDE = 8
NODES = 384
C4 = 98
C2 = 26
CYCLES = 2
GX = 16
GY = 8
GZ = 32


def shared_matrices(key):
    base = jax.random.fold_in(key, 7)
    keys = jax.random.split(base, 4)
    spread = 0.5
    gauss = jax.random.normal(keys[0], (NODES, NODES), jnp.float32) * spread / jnp.sqrt(jnp.float32(NODES))
    offdiag = (gauss + gauss.T) * (1.0 - jnp.eye(NODES, dtype=jnp.float32))
    diagonal = jnp.sum(jnp.abs(offdiag), axis=1) + jax.random.uniform(keys[1], (NODES,), jnp.float32, 0.5, 2.0)
    matrix = (offdiag + jnp.diag(diagonal)) / 8.0
    inverse = jnp.linalg.inv(matrix)
    prolong_four = jax.random.normal(keys[2], (NODES, C4), jnp.float32) / jnp.sqrt(jnp.float32(C4))
    prolong_two = jax.random.normal(keys[3], (NODES, C2), jnp.float32) / jnp.sqrt(jnp.float32(C2))
    galerkin_four = jnp.dot(jnp.dot(prolong_four.T, matrix, precision=lax.Precision.HIGHEST), prolong_four, precision=lax.Precision.HIGHEST)
    galerkin_two = jnp.dot(jnp.dot(prolong_two.T, matrix, precision=lax.Precision.HIGHEST), prolong_two, precision=lax.Precision.HIGHEST)
    return (matrix, inverse, prolong_four, jnp.linalg.inv(galerkin_four), prolong_two, jnp.linalg.inv(galerkin_two))


def draw_fine_matrix(key, part):
    return shared_matrices(key)[0]


def draw_fine_inverse(key, part):
    return shared_matrices(key)[1]


def draw_prolong_four(key, part):
    return shared_matrices(key)[2]


def draw_coarse_four(key, part):
    return shared_matrices(key)[3]


def draw_prolong_two(key, part):
    return shared_matrices(key)[4]


def draw_coarse_two(key, part):
    return shared_matrices(key)[5]


def plant(values, key, least, top_value):
    longest = values.shape.index(max(values.shape))
    spots = []
    for shift in (0, 1):
        where = [jax.random.randint(jax.random.fold_in(key, axis), (), 0, length) for axis, length in enumerate(values.shape)]
        where[longest] = (where[longest] + shift) % values.shape[longest]
        spots.append(tuple(where))
    return values.at[spots[0]].set(least).at[spots[1]].set(top_value)


def shard_levels(stream_key, extent, cuts, low, top_value):
    def one(dim, blocks):
        draws = jax.random.uniform(jax.random.fold_in(jax.random.fold_in(stream_key, 6), dim), (blocks,), jnp.float32, low / len(cuts), top_value / len(cuts))
        return jnp.repeat(jnp.exp(draws), extent[dim] // blocks).reshape((-1,) + (1,) * (len(extent) - dim - 1))

    gain = one(*cuts[0])
    for cut in cuts[1:]:
        gain = gain * one(*cut)
    return gain


def bell_draw(rng, shape, scale, limit, cuts=(), kind=jnp.bfloat16):
    level = shard_levels(rng, shape, cuts, -0.22, 0.18) if cuts else 1.0
    result = jax.random.normal(rng, shape, jnp.float32) * scale * level
    return jnp.minimum(jnp.maximum(result, -limit), limit).astype(kind)


def setup_inputs(seed: int = 0) -> dict:
    arg_keys = jax.random.split(jax.random.key(seed), 11)
    return {
        "load_raw": bell_draw(arg_keys[0], (GX, GY, GZ, SPECIES, NODES), 1.0, 8.0, ((0, 8), (1, 4), (2, 8)), jnp.float32),
        "scaling": jnp.clip(jnp.exp(math.log(1.8) - 1.0986122 * jax.random.uniform(arg_keys[1], (GX, GY, GZ, NODES), jnp.float32) ** shard_levels(arg_keys[1], (GX, GY, GZ, NODES), ((0, 8), (1, 4), (2, 8)), -0.2, 0.2)), 0.6, 1.8),
        "fine_matrix": draw_fine_matrix(jax.random.fold_in(arg_keys[10], 71), 0),
        "fine_inverse": draw_fine_inverse(jax.random.fold_in(arg_keys[10], 71), 0),
        "prolong_four": draw_prolong_four(jax.random.fold_in(arg_keys[10], 71), 0),
        "coarse_four": draw_coarse_four(jax.random.fold_in(arg_keys[10], 71), 0),
        "prolong_two": draw_prolong_two(jax.random.fold_in(arg_keys[10], 71), 0),
        "coarse_two": draw_coarse_two(jax.random.fold_in(arg_keys[10], 71), 0),
        "orient": plant(jax.random.randint(arg_keys[8], (3, GX, GY, GZ), 0, 4), jax.random.fold_in(arg_keys[8], 1), 0, 3).astype(jnp.int32),
        "boundary": plant(jax.random.randint(arg_keys[9], (6, GX, GY, GZ), 0, 2), jax.random.fold_in(arg_keys[9], 1), 0, 1).astype(jnp.int32),
    }


fine_weight = 0.5
coarse_weight = 0.5

def flip_face(face_data, face_code):
    reshaped = face_data.reshape(face_data.shape[:-1] + (FACE_SIDE, FACE_SIDE))
    codes_full = face_code[:, :, :, None, None, None]
    reshaped = jnp.where(codes_full % 2 == 1, jnp.flip(reshaped, -2), reshaped)
    reshaped = jnp.where(codes_full // 2 == 1, jnp.flip(reshaped, -1), reshaped)
    return reshaped.reshape(face_data.shape)

def keep_factors(boundary, dim_index, count_along):
    position = lax.broadcasted_iota(jnp.int32, boundary.shape[1:], dim_index)
    keep_low = 1 - jnp.where(position == 0, boundary[2 * dim_index], 0)
    keep_top = 1 - jnp.where(position == count_along - 1, boundary[2 * dim_index + 1], 0)
    return (keep_low.astype(jnp.float32), keep_top.astype(jnp.float32))

def assemble(element_data, orient, boundary):
    face_nodes = FACE_SIDE * FACE_SIDE
    face_list = [element_data[..., face_index * face_nodes:(face_index + 1) * face_nodes] for face_index in range(6)]
    pieces = []
    for dim_index in range(3):
        low_face = face_list[2 * dim_index]
        top_face = face_list[2 * dim_index + 1]
        face_code = orient[dim_index]
        count_along = low_face.shape[dim_index]
        sent_low = flip_face(low_face, face_code)
        zero_slab = jnp.zeros_like(lax.slice_in_dim(low_face, 0, 1, axis=dim_index))
        above = jnp.concatenate([lax.slice_in_dim(sent_low, 1, count_along, axis=dim_index), zero_slab], dim_index)
        below = flip_face(jnp.concatenate([zero_slab, lax.slice_in_dim(top_face, 0, count_along - 1, axis=dim_index)], dim_index), face_code)
        keep_low, keep_top = keep_factors(boundary, dim_index, count_along)
        pieces.append((low_face + below) * keep_low[:, :, :, None, None])
        pieces.append((top_face + above) * keep_top[:, :, :, None, None])
    return jnp.concatenate(pieces, -1)

def product(left, right):
    return jnp.dot(left.astype(jnp.float32), right.astype(jnp.float32), precision=lax.Precision.HIGHEST, preferred_element_type=jnp.float32)

def apply_operator(solution, scaling, fine_matrix):
    scaled = solution * scaling[:, :, :, None, :]
    row_block = product(scaled.reshape(-1, NODES), fine_matrix).reshape(solution.shape)
    return row_block * scaling[:, :, :, None, :]

def smooth_terms(residual, scaling, fine_inverse, prolong_four, coarse_four, prolong_two, coarse_two):
    scaled = (residual / scaling[:, :, :, None, :]).reshape(-1, NODES)
    fine_term = fine_weight * product(scaled, fine_inverse)
    four_term = coarse_weight * product(product(product(scaled, prolong_four), coarse_four), prolong_four.T)
    two_term = coarse_weight * product(product(product(scaled, prolong_two), coarse_two), prolong_two.T)
    inverse_scale = 1.0 / scaling[:, :, :, None, :]
    return (fine_term.reshape(residual.shape) * inverse_scale, four_term.reshape(residual.shape) * inverse_scale, two_term.reshape(residual.shape) * inverse_scale)

def reference(load_raw, scaling, fine_matrix, fine_inverse, prolong_four, coarse_four, prolong_two, coarse_two, orient, boundary):
    assembled = assemble(load_raw, orient, boundary)
    solution = jnp.zeros_like(load_raw)
    for cycle_index in range(CYCLES):
        if cycle_index == 0:
            residual = assembled
        else:
            residual = assembled - assemble(apply_operator(solution, scaling, fine_matrix), orient, boundary)
        terms = smooth_terms(residual, scaling, fine_inverse, prolong_four, coarse_four, prolong_two, coarse_two)
        solution = solution + assemble(terms[0] + terms[1] + terms[2], orient, boundary)
    return solution
```

```python
import jax
import jax.numpy as jnp
from jax import lax
from jax.experimental import pallas as pl
from jax.experimental.pallas import tpu as pltpu
from jax.sharding import PartitionSpec as P

CYCLES = 2
ROUNDS = 2 * CYCLES
HALVES = 2
AXES = ("ex", "ey", "ez")

fine_weight = 0.5
coarse_weight = 0.5


def parts_of(value):
    high = value.astype(jnp.bfloat16)
    low = (value - high.astype(jnp.float32)).astype(jnp.bfloat16)
    return high, low


def small_dot(left, right):
    left_high, left_low = parts_of(left)
    right_high, right_low = parts_of(right)

    def one(a, b):
        return jnp.dot(a, b, preferred_element_type=jnp.float32)

    return one(left_high, right_high) + one(left_low, right_high) + one(left_high, right_low)


def kernel(
    load_hbm, fine_matrix_hbm, fine_inverse_hbm, scaling_ref, prolong_four_ref, coarse_four_ref, prolong_two_ref,
    coarse_two_ref, orient_ref, boundary_ref,
    out_hbm,
    load_v, out_v, y_v, swapped_v, assembled_v, first_v, matrix_v, operator_v, smoother_v,
    index_v, face_index_v, keep_inverse_v, inverse_v, keep_scale_v, scale_v, keep_v,
    sent_xy, sent_z, got_xy, got_z,
    load_sem, matrix_sem, out_sem, send_sem, recv_sem,
):
    groups = load_v.shape[1] // HALVES
    position = [lax.axis_index(axis) for axis in AXES]
    size = [lax.axis_size(axis) for axis in AXES]
    has_below = [position[a] > 0 for a in range(3)]
    has_above = [position[a] < size[a] - 1 for a in range(3)]

    def load_copy(half):
        rows = pl.ds(half * groups, groups)
        return pltpu.make_async_copy(load_hbm.at[:, rows], load_v.at[:, rows], load_sem.at[half])

    def out_copy(half):
        rows = pl.ds(half * groups, groups)
        return pltpu.make_async_copy(out_v.at[:, rows], out_hbm.at[:, rows], out_sem.at[half])

    fine_inverse_copy = pltpu.make_async_copy(fine_inverse_hbm, matrix_v.at[0], matrix_sem.at[0])
    fine_matrix_copy = pltpu.make_async_copy(fine_matrix_hbm, matrix_v.at[1], matrix_sem.at[1])
    for half in range(HALVES):
        load_copy(half).start()
    fine_inverse_copy.start()
    fine_matrix_copy.start()

    barrier = pltpu.get_barrier_semaphore()
    for a in range(3):
        for there, step in ((has_below[a], -1), (has_above[a], 1)):

            @pl.when(there)
            def _():
                pl.semaphore_signal(
                    barrier, inc=1, device_id={AXES[a]: position[a] + step}, device_id_type=pl.DeviceIdType.MESH
                )

    lane = lax.broadcasted_iota(jnp.int32, (8, 128), 1)
    lower_half = lane < 64

    def mask_of(a, i, j, k):
        code = orient_ref[a, i, j, k]
        return (code & 1) * 56 + (code >> 1) * 7

    for i in range(2):
        for j in range(2):
            for k in range(4):
                e = (i * 2 + j) * 4 + k
                for a in range(3):
                    above = [i, j, k]
                    above[a] += 1
                    own = mask_of(a, i, j, k)
                    if above[a] < (2, 2, 4)[a]:
                        bits = jnp.where(lower_half, mask_of(a, *above), own)
                    else:
                        bits = jnp.full((8, 128), own, jnp.int32)
                    index_v[a, e] = (lane ^ 64) ^ bits
                    if (i, j, k)[a] == 0:
                        parity = j if a == 2 else k % 2
                        slot = (j * 4 + k, i * 4 + k, i * 2 + j)[a]
                        face_index_v[a, slot] = lane ^ (own ^ (64 * parity))

                row = jnp.broadcast_to(scaling_ref[i, j, k : k + 1, :], (8, scaling_ref.shape[-1]))
                inverse = 1.0 / row
                keeps = []
                for a in range(3):
                    low_zero = jnp.where((i, j, k)[a] == 0, jnp.where(position[a] == 0, boundary_ref[i, j, k, 2 * a], 0), 0)
                    at_top = (i, j, k)[a] == (2, 2, 4)[a] - 1
                    top_zero = jnp.where(at_top, jnp.where(position[a] == size[a] - 1, boundary_ref[i, j, k, 2 * a + 1], 0), 0)
                    keeps.append((1 - jnp.where(lower_half, low_zero, top_zero)).astype(jnp.float32))
                keep = jnp.concatenate(keeps, -1)
                scale_v[e] = row
                inverse_v[e] = inverse
                keep_scale_v[e] = keep * row
                keep_inverse_v[e] = keep * inverse
                keep_v[e] = keep

    for a in range(3):
        for there, direction in ((has_above[a], 0), (has_below[a], 1)):

            @pl.when(jnp.logical_not(there))
            def _():
                for turn in range(ROUNDS):
                    for half in range(HALVES):
                        if a < 2:
                            got_xy[turn, half, 2 * a + direction] = jnp.zeros(got_xy.shape[3:], jnp.float32)
                        else:
                            got_z[turn, half, direction] = jnp.zeros(got_z.shape[3:], jnp.float32)

    def face_copy(turn, half, a, direction):
        channel = 2 * a + direction
        if a < 2:
            source, target = sent_xy.at[turn, half, channel], got_xy.at[turn, half, channel]
        else:
            source, target = sent_z.at[turn, half, direction], got_z.at[turn, half, direction]
        return pltpu.make_async_remote_copy(
            source, target, send_sem.at[turn, half, channel], recv_sem.at[turn, half, channel],
            device_id={AXES[a]: position[a] + (1 if direction else -1)}, device_id_type=pl.DeviceIdType.MESH,
        )

    def rolled(value):
        return pltpu.roll(value.reshape(-1, 128), 64, 1).reshape(value.shape)

    def gathered(value, index):
        index = jnp.broadcast_to(index, value.shape)
        return jnp.take_along_axis(
            value.reshape(-1, 128), index.reshape(-1, 128), axis=1, mode="promise_in_bounds"
        ).reshape(value.shape)

    def edge(value, a, last):
        layer = lax.index_in_dim(value, -1 if last else 0, a, keepdims=False)
        if a < 2:
            layer = layer.reshape((2, 2, 2) + layer.shape[2:])
            return layer[:, :, 0], layer[:, :, 1]
        return layer[:, 0], layer[:, 1]

    def packed(pair):
        first, second = pair
        return jnp.where(lower_half, rolled(first), second)

    def shaped(value):
        return value.reshape((2, 2, 4) + value.shape[1:])

    def send(turn, half, source, a):
        swapped = gathered(source, index_v[a][:, None])
        swapped_v[half, a] = swapped
        down = packed(edge(shaped(swapped), a, False))
        up = packed(edge(shaped(source), a, True))
        if a < 2:
            sent_xy[turn, half, 2 * a] = down.reshape(sent_xy.shape[3:])
            sent_xy[turn, half, 2 * a + 1] = up.reshape(sent_xy.shape[3:])
        else:
            sent_z[turn, half, 0] = down.reshape(sent_z.shape[3:])
            sent_z[turn, half, 1] = up.reshape(sent_z.shape[3:])
        for there, direction in ((has_below[a], 0), (has_above[a], 1)):

            @pl.when(there)
            def _():
                face_copy(turn, half, a, direction).start()

    def receive(turn, half):
        for a in range(3):

            @pl.when(has_below[a])
            def _():
                face_copy(turn, half, a, 0).wait_send()
                face_copy(turn, half, a, 1).wait_recv()

            @pl.when(has_above[a])
            def _():
                face_copy(turn, half, a, 1).wait_send()
                face_copy(turn, half, a, 0).wait_recv()

    def assembled_sum(turn, half, source, a):
        swapped = shaped(swapped_v[half, a])
        if a < 2:
            down, up = got_xy[turn, half, 2 * a], got_xy[turn, half, 2 * a + 1]
            lead = (2, 2)
        else:
            down, up = got_z[turn, half, 0], got_z[turn, half, 1]
            lead = (2,)
        face_index = face_index_v[a, : 4 if a == 2 else 8].reshape(lead + (2, 8, 128))
        wide = lead + down.shape[1:]
        down, up = down.reshape(wide), up.reshape(wide)
        top = jnp.stack([rolled(down), down], len(lead))
        low = jnp.stack(
            [gathered(up, lax.index_in_dim(face_index, parity, len(lead), keepdims=True)) for parity in range(2)],
            len(lead),
        )
        layer = list(swapped.shape)
        layer[a] = 1
        top, low = top.reshape(layer), low.reshape(layer)
        count = swapped.shape[a]
        from_below = jnp.concatenate([low, lax.slice_in_dim(swapped, 0, count - 1, axis=a)], a)
        from_above = jnp.concatenate([lax.slice_in_dim(swapped, 1, count, axis=a), top], a)
        return source + jnp.where(lower_half, from_below, from_above).reshape(source.shape)

    def columns(a):
        return slice(a * 128, (a + 1) * 128)

    def multiply_and_send(turn, half, row_parts, matrix_ref, factor_ref):
        high, low = (jnp.concatenate(parts, -1) for parts in zip(*row_parts))
        rows = jnp.concatenate([high, low, high], -1)
        for span in ((0, 2), (2, 3)):
            wide = slice(span[0] * 128, span[1] * 128)
            out = jnp.dot(rows, matrix_ref[:, wide], preferred_element_type=jnp.float32)
            for a in range(*span):
                piece = out[:, (a - span[0]) * 128 : (a - span[0] + 1) * 128].reshape(16, groups, 8, 128)
                piece = piece * factor_ref[:, :, columns(a)][:, None]
                y_v[half, a] = piece
                send(turn, half, piece, a)

    def half_rows(ref, half, a):
        return ref[:, half * groups : (half + 1) * groups, :, columns(a)]

    pl.semaphore_wait(barrier, sum(there.astype(jnp.int32) for there in has_below + has_above))

    for half in range(HALVES):
        load_copy(half).wait()
        for a in range(3):
            send(0, half, half_rows(load_v, half, a), a)

    coarse = small_dot(
        prolong_four_ref[...].T, small_dot(coarse_four_ref[...], prolong_four_ref[...])
    ) + small_dot(prolong_two_ref[...].T, small_dot(coarse_two_ref[...], prolong_two_ref[...]))
    fine_inverse_copy.wait()
    smoother_high, smoother_low = parts_of(fine_weight * matrix_v[0] + coarse_weight * coarse)
    nodes = smoother_high.shape[0]
    smoother_v[:nodes] = smoother_high
    smoother_v[nodes : 2 * nodes] = smoother_high
    smoother_v[2 * nodes :] = smoother_low
    fine_matrix_copy.wait()
    operator_high, operator_low = parts_of(matrix_v[1])
    operator_v[:nodes] = operator_high
    operator_v[nodes : 2 * nodes] = operator_high
    operator_v[2 * nodes :] = operator_low

    def flat_parts(value):
        return parts_of(value.reshape(-1, 128))

    for half in range(HALVES):
        receive(0, half)
        row_parts = []
        for a in range(3):
            total = assembled_sum(0, half, half_rows(load_v, half, a), a)
            assembled_v[half, a] = total
            row_parts.append(flat_parts(total * keep_inverse_v[:, :, columns(a)][:, None]))
        multiply_and_send(1, half, row_parts, smoother_v, inverse_v)
    for half in range(HALVES):
        receive(1, half)
        row_parts = []
        for a in range(3):
            total = assembled_sum(1, half, y_v[half, a], a)
            first_v[half, a] = total
            row_parts.append(flat_parts(total * keep_scale_v[:, :, columns(a)][:, None]))
        multiply_and_send(2, half, row_parts, operator_v, scale_v)
    for half in range(HALVES):
        receive(2, half)
        row_parts = []
        for a in range(3):
            total = assembled_v[half, a] - assembled_sum(2, half, y_v[half, a], a)
            row_parts.append(flat_parts(total * keep_inverse_v[:, :, columns(a)][:, None]))
        multiply_and_send(3, half, row_parts, smoother_v, inverse_v)
    for half in range(HALVES):
        receive(3, half)
        for a in range(3):
            total = first_v[half, a] + assembled_sum(3, half, y_v[half, a], a)
            out_v[:, half * groups : (half + 1) * groups, :, columns(a)] = total * keep_v[:, :, columns(a)][:, None]
        out_copy(half).start()
    for half in range(HALVES):
        out_copy(half).wait()


def body(
    load_raw, scaling, fine_matrix, fine_inverse, prolong_four, coarse_four, prolong_two, coarse_two, orient, boundary
):
    nodes = load_raw.shape[-1]
    groups = load_raw.shape[3] // 8
    local = groups // HALVES
    elements = 16
    f32, bf16 = jnp.float32, jnp.bfloat16
    vmem = pl.BlockSpec(memory_space=pltpu.VMEM)
    smem = pl.BlockSpec(memory_space=pltpu.SMEM)
    anywhere = pl.BlockSpec(memory_space=pl.ANY)
    per_half = pltpu.VMEM((HALVES, 3, elements, local, 8, 128), f32)
    factor = pltpu.VMEM((elements, 8, nodes), f32)
    out = pl.pallas_call(
        kernel,
        out_shape=jax.ShapeDtypeStruct((elements, groups, 8, nodes), f32),
        in_specs=[anywhere] * 3 + [vmem] * 5 + [smem] * 2,
        out_specs=anywhere,
        scratch_shapes=[
            pltpu.VMEM((elements, groups, 8, nodes), f32),
            pltpu.VMEM((elements, groups, 8, nodes), f32),
            per_half, per_half, per_half, per_half,
            pltpu.VMEM((2, nodes, nodes), f32),
            pltpu.VMEM((3 * nodes, nodes), bf16),
            pltpu.VMEM((3 * nodes, nodes), bf16),
            pltpu.VMEM((3, elements, 8, 128), jnp.int32),
            pltpu.VMEM((3, 8, 8, 128), jnp.int32),
            factor, factor, factor, factor, factor,
            pltpu.VMEM((ROUNDS, HALVES, 4, 4, local, 8, 128), f32),
            pltpu.VMEM((ROUNDS, HALVES, 2, 2, local, 8, 128), f32),
            pltpu.VMEM((ROUNDS, HALVES, 4, 4, local, 8, 128), f32),
            pltpu.VMEM((ROUNDS, HALVES, 2, 2, local, 8, 128), f32),
            pltpu.SemaphoreType.DMA((HALVES,)),
            pltpu.SemaphoreType.DMA((2,)),
            pltpu.SemaphoreType.DMA((HALVES,)),
            pltpu.SemaphoreType.DMA((ROUNDS, HALVES, 6)),
            pltpu.SemaphoreType.DMA((ROUNDS, HALVES, 6)),
        ],
        compiler_params=pltpu.CompilerParams(collective_id=0, has_side_effects=True),
    )(
        load_raw.reshape(elements, groups, 8, nodes), fine_matrix, fine_inverse, scaling, prolong_four.T, coarse_four,
        prolong_two.T, coarse_two, orient, boundary.transpose(1, 2, 3, 0),
    )
    return out.reshape(load_raw.shape)


def solution(mesh):
    in_specs = (
        P("ex", "ey", "ez", None, None),
        P("ex", "ey", "ez", None),
        P(),
        P(),
        P(),
        P(),
        P(),
        P(),
        P(None, "ex", "ey", "ez"),
        P(None, "ex", "ey", "ez"),
    )
    out_specs = P("ex", "ey", "ez", None, None)
    return jax.shard_map(body, mesh=mesh, in_specs=in_specs, out_specs=out_specs, check_vma=False)
```

```python
import jax
import jax.numpy as jnp
from jax import lax
from jax.experimental import pallas as pl
from jax.experimental.pallas import tpu as pltpu
from jax.sharding import PartitionSpec as P

CYCLES = 2
ROUNDS = 2 * CYCLES
HALVES = 2
AXES = ("ex", "ey", "ez")
GROUPS = ((0, 1, 2),)

fine_weight = 0.5
coarse_weight = 0.5


def parts_of(value):
    high = value.astype(jnp.bfloat16)
    low = (value - high.astype(jnp.float32)).astype(jnp.bfloat16)
    return high, low


def small_dot(left, right):
    left_high, left_low = parts_of(left)
    right_high, right_low = parts_of(right)

    def one(a, b):
        return jnp.dot(a, b, preferred_element_type=jnp.float32)

    return one(left_high, right_high) + one(left_low, right_high) + one(left_high, right_low)


def kernel(
    load_hbm, fine_matrix_hbm, fine_inverse_hbm, scaling_hbm, prolong_four_hbm, coarse_four_hbm, prolong_two_hbm,
    coarse_two_hbm, orient_hbm, boundary_hbm,
    out_ref,
    load_v, y_v, swapped_v, assembled_v, first_v, matrix_v, operator_v, smoother_v,
    scaling_ref, prolong_four_ref, coarse_four_ref, prolong_two_ref, coarse_two_ref, orient_ref, boundary_ref,
    index_v, face_index_v, keep_inverse_v, inverse_v, keep_scale_v, scale_v, keep_v,
    sent_xy, sent_z, got_xy, got_z,
    load_sem, small_sem, send_sem, recv_sem,
):
    groups = load_v.shape[1] // HALVES
    position = [lax.axis_index(axis) for axis in AXES]
    size = [lax.axis_size(axis) for axis in AXES]
    has_below = [position[a] > 0 for a in range(3)]
    has_above = [position[a] < size[a] - 1 for a in range(3)]

    def load_copy(half):
        rows = pl.ds(half * groups, groups)
        return pltpu.make_async_copy(load_hbm.at[:, rows], load_v.at[:, rows], load_sem.at[half])

    barrier = pltpu.get_barrier_semaphore()
    for a in range(3):
        for there, step in ((has_below[a], -1), (has_above[a], 1)):

            @pl.when(there)
            def _():
                pl.semaphore_signal(
                    barrier, inc=1, device_id={AXES[a]: position[a] + step}, device_id_type=pl.DeviceIdType.MESH
                )

    small = [
        pltpu.make_async_copy(source, target, small_sem.at[n])
        for n, (source, target) in enumerate(
            (
                (orient_hbm, orient_ref),
                (boundary_hbm, boundary_ref),
                (scaling_hbm, scaling_ref),
                (coarse_four_hbm, coarse_four_ref),
                (prolong_four_hbm, prolong_four_ref),
                (coarse_two_hbm, coarse_two_ref),
                (prolong_two_hbm, prolong_two_ref),
                (fine_inverse_hbm, matrix_v.at[0]),
                (fine_matrix_hbm, matrix_v.at[1]),
            )
        )
    ]
    small[0].start()
    for half in range(HALVES):
        load_copy(half).start()
    for copy in small[1:]:
        copy.start()

    lane = lax.broadcasted_iota(jnp.int32, (8, 128), 1)
    lower_half = lane < 64

    small[0].wait()

    def mask_of(a, i, j, k):
        code = orient_ref[a, i, j, k]
        return (code & 1) * 56 + (code >> 1) * 7

    for i in range(2):
        for j in range(2):
            for k in range(4):
                e = (i * 2 + j) * 4 + k
                for a in range(3):
                    above = [i, j, k]
                    above[a] += 1
                    own = mask_of(a, i, j, k)
                    if above[a] < (2, 2, 4)[a]:
                        bits = jnp.where(lower_half, mask_of(a, *above), own)
                    else:
                        bits = jnp.where(lower_half, 0, own)
                    index_v[a, e] = (lane ^ 64) ^ bits
                    if (i, j, k)[a] == 0:
                        parity = j if a == 2 else k % 2
                        slot = (j * 4 + k, i * 4 + k, i * 2 + j)[a]
                        face_index_v[a, slot] = lane ^ (own ^ (64 * parity))

    for a in range(3):
        for there, direction in ((has_above[a], 0), (has_below[a], 1)):

            @pl.when(jnp.logical_not(there))
            def _():
                for turn in range(ROUNDS):
                    for half in range(HALVES):
                        if a < 2:
                            got_xy[turn, half, 2 * a + direction] = jnp.zeros(got_xy.shape[3:], jnp.float32)
                        else:
                            got_z[turn, half, direction] = jnp.zeros(got_z.shape[3:], jnp.float32)

    def face_copy(turn, half, a, direction):
        channel = 2 * a + direction
        if a < 2:
            source, target = sent_xy.at[turn, half, channel], got_xy.at[turn, half, channel]
        else:
            source, target = sent_z.at[turn, half, direction], got_z.at[turn, half, direction]
        return pltpu.make_async_remote_copy(
            source, target, send_sem.at[turn, half, channel], recv_sem.at[turn, half, channel],
            device_id={AXES[a]: position[a] + (1 if direction else -1)}, device_id_type=pl.DeviceIdType.MESH,
        )

    def rolled(value):
        return pltpu.roll(value.reshape(-1, 128), 64, 1).reshape(value.shape)

    def gathered(value, index):
        index = jnp.broadcast_to(index, value.shape)
        return jnp.take_along_axis(
            value.reshape(-1, 128), index.reshape(-1, 128), axis=1, mode="promise_in_bounds"
        ).reshape(value.shape)

    def edge(value, a, last):
        layer = lax.index_in_dim(value, -1 if last else 0, a, keepdims=False)
        if a < 2:
            layer = layer.reshape((2, 2, 2) + layer.shape[2:])
            return layer[:, :, 0], layer[:, :, 1]
        return layer[:, 0], layer[:, 1]

    def shaped(value):
        return value.reshape((2, 2, 4) + value.shape[1:])

    def pack(turn, half, source, a):
        swapped = gathered(source, index_v[a][:, None])
        swapped_v[half, a] = swapped
        first, second = edge(shaped(swapped), a, False)
        down = jnp.where(lower_half, rolled(first), second)
        up = jnp.where(lower_half, edge(shaped(swapped), a, True)[0], edge(shaped(source), a, True)[1])
        if a < 2:
            sent_xy[turn, half, 2 * a] = down.reshape(sent_xy.shape[3:])
            sent_xy[turn, half, 2 * a + 1] = up.reshape(sent_xy.shape[3:])
        else:
            sent_z[turn, half, 0] = down.reshape(sent_z.shape[3:])
            sent_z[turn, half, 1] = up.reshape(sent_z.shape[3:])

    def send(turn, half, a):
        for there, direction in ((has_below[a], 0), (has_above[a], 1)):

            @pl.when(there)
            def _():
                face_copy(turn, half, a, direction).start()

    def receive(turn, half):
        for a in range(3):

            @pl.when(has_below[a])
            def _():
                face_copy(turn, half, a, 0).wait_send()
                face_copy(turn, half, a, 1).wait_recv()

            @pl.when(has_above[a])
            def _():
                face_copy(turn, half, a, 1).wait_send()
                face_copy(turn, half, a, 0).wait_recv()

    def assembled_sum(turn, half, source, a):
        swapped = shaped(swapped_v[half, a])
        if a < 2:
            down, up = got_xy[turn, half, 2 * a], got_xy[turn, half, 2 * a + 1]
            lead = (2, 2)
        else:
            down, up = got_z[turn, half, 0], got_z[turn, half, 1]
            lead = (2,)
        face_index = face_index_v[a, : 4 if a == 2 else 8].reshape(lead + (2, 8, 128))
        wide = lead + down.shape[1:]
        down, up = down.reshape(wide), up.reshape(wide)
        top = jnp.stack([rolled(down), down], len(lead))
        low = jnp.stack(
            [gathered(up, lax.index_in_dim(face_index, parity, len(lead), keepdims=True)) for parity in range(2)],
            len(lead),
        )
        layer = list(swapped.shape)
        layer[a] = 1
        top, low = top.reshape(layer), low.reshape(layer)
        count = swapped.shape[a]
        from_below = jnp.concatenate([low, lax.slice_in_dim(swapped, 0, count - 1, axis=a)], a)
        from_above = jnp.concatenate([lax.slice_in_dim(swapped, 1, count, axis=a), top], a)
        return source + jnp.where(lower_half, from_below, from_above).reshape(source.shape)

    def columns(a):
        return slice(a * 128, (a + 1) * 128)

    def multiply_and_send(turn, half, row_parts, matrix_ref, factor_ref):
        rows = jnp.concatenate([part for parts in row_parts for part in parts], -1)
        for group in GROUPS:
            for a in group:
                out = jnp.dot(rows, matrix_ref[a], preferred_element_type=jnp.float32)
                out = out[:, :128] + out[:, 128:]
                piece = out.reshape(16, groups, 8, 128) * factor_ref[:, :, columns(a)][:, None]
                y_v[half, a] = piece
                pack(turn, half, piece, a)
            for a in group:
                send(turn, half, a)

    def set_matrix(value, matrix_ref):
        high, low = parts_of(value)
        for a in range(3):
            for b in range(3):
                block = jnp.concatenate(
                    [part[b * 128 : (b + 1) * 128, a * 128 : (a + 1) * 128] for part in (high, low)], -1
                )
                matrix_ref[a, 2 * b * 128 : (2 * b + 1) * 128] = block
                matrix_ref[a, (2 * b + 1) * 128 : (2 * b + 2) * 128] = block

    def half_rows(ref, half, a):
        return ref[:, half * groups : (half + 1) * groups, :, columns(a)]

    pl.semaphore_wait(barrier, sum(there.astype(jnp.int32) for there in has_below + has_above))

    for half in range(HALVES):
        load_copy(half).wait()
        for a in range(3):
            pack(0, half, half_rows(load_v, half, a), a)
        for a in range(3):
            send(0, half, a)

    small[1].wait()
    small[2].wait()
    for i in range(2):
        for j in range(2):
            for k in range(4):
                e = (i * 2 + j) * 4 + k
                row = jnp.broadcast_to(scaling_ref[i, j, k : k + 1, :], (8, scaling_ref.shape[-1]))
                inverse = 1.0 / row
                keeps = []
                for a in range(3):
                    low_zero = jnp.where((i, j, k)[a] == 0, jnp.where(position[a] == 0, boundary_ref[i, j, k, 2 * a], 0), 0)
                    at_top = (i, j, k)[a] == (2, 2, 4)[a] - 1
                    top_zero = jnp.where(at_top, jnp.where(position[a] == size[a] - 1, boundary_ref[i, j, k, 2 * a + 1], 0), 0)
                    keeps.append((1 - jnp.where(lower_half, low_zero, top_zero)).astype(jnp.float32))
                keep = jnp.concatenate(keeps, -1)
                scale_v[e] = row
                inverse_v[e] = inverse
                keep_scale_v[e] = keep * row
                keep_inverse_v[e] = keep * inverse
                keep_v[e] = keep

    for copy in small[3:8]:
        copy.wait()
    coarse = small_dot(
        prolong_four_ref[...].T, small_dot(coarse_four_ref[...], prolong_four_ref[...])
    ) + small_dot(prolong_two_ref[...].T, small_dot(coarse_two_ref[...], prolong_two_ref[...]))
    set_matrix(fine_weight * matrix_v[0] + coarse_weight * coarse, smoother_v)
    small[8].wait()
    set_matrix(matrix_v[1], operator_v)

    def flat_parts(value):
        return parts_of(value.reshape(-1, 128))

    for half in range(HALVES):
        receive(0, half)
        row_parts = []
        for a in range(3):
            total = assembled_sum(0, half, half_rows(load_v, half, a), a)
            assembled_v[half, a] = total
            row_parts.append(flat_parts(total * keep_inverse_v[:, :, columns(a)][:, None]))
        multiply_and_send(1, half, row_parts, smoother_v, inverse_v)
    for half in range(HALVES):
        receive(1, half)
        row_parts = []
        for a in range(3):
            total = assembled_sum(1, half, y_v[half, a], a)
            first_v[half, a] = total
            row_parts.append(flat_parts(total * keep_scale_v[:, :, columns(a)][:, None]))
        multiply_and_send(2, half, row_parts, operator_v, scale_v)
    for half in range(HALVES):
        receive(2, half)
        row_parts = []
        for a in range(3):
            total = assembled_v[half, a] - assembled_sum(2, half, y_v[half, a], a)
            row_parts.append(flat_parts(total * keep_inverse_v[:, :, columns(a)][:, None]))
        multiply_and_send(3, half, row_parts, smoother_v, inverse_v)
    for half in range(HALVES):
        receive(3, half)
        for a in range(3):
            total = first_v[half, a] + assembled_sum(3, half, y_v[half, a], a)
            out_ref[:, half * groups : (half + 1) * groups, :, columns(a)] = total * keep_v[:, :, columns(a)][:, None]


def body(
    load_raw, scaling, fine_matrix, fine_inverse, prolong_four, coarse_four, prolong_two, coarse_two, orient, boundary
):
    nodes = load_raw.shape[-1]
    groups = load_raw.shape[3] // 8
    local = groups // HALVES
    elements = 16
    f32, bf16 = jnp.float32, jnp.bfloat16
    per_half = pltpu.VMEM((HALVES, 3, elements, local, 8, 128), f32)
    factor = pltpu.VMEM((elements, 8, nodes), f32)
    out = pl.pallas_call(
        kernel,
        out_shape=pltpu.VMEM((elements, groups, 8, nodes), f32),
        in_specs=[pl.BlockSpec(memory_space=pltpu.HBM)] * 10,
        out_specs=pl.BlockSpec(memory_space=pltpu.VMEM),
        scratch_shapes=[
            pltpu.VMEM((elements, groups, 8, nodes), f32),
            per_half, per_half, per_half, per_half,
            pltpu.VMEM((2, nodes, nodes), f32),
            pltpu.VMEM((3, 2 * nodes, 256), bf16),
            pltpu.VMEM((3, 2 * nodes, 256), bf16),
            pltpu.VMEM(scaling.shape, f32),
            pltpu.VMEM(prolong_four.shape[::-1], f32),
            pltpu.VMEM(coarse_four.shape, f32),
            pltpu.VMEM(prolong_two.shape[::-1], f32),
            pltpu.VMEM(coarse_two.shape, f32),
            pltpu.SMEM(orient.shape, jnp.int32),
            pltpu.SMEM(boundary.shape[1:] + boundary.shape[:1], jnp.int32),
            pltpu.VMEM((3, elements, 8, 128), jnp.int32),
            pltpu.VMEM((3, 8, 8, 128), jnp.int32),
            factor, factor, factor, factor, factor,
            pltpu.VMEM((ROUNDS, HALVES, 4, 4, local, 8, 128), f32),
            pltpu.VMEM((ROUNDS, HALVES, 2, 2, local, 8, 128), f32),
            pltpu.VMEM((ROUNDS, HALVES, 4, 4, local, 8, 128), f32),
            pltpu.VMEM((ROUNDS, HALVES, 2, 2, local, 8, 128), f32),
            pltpu.SemaphoreType.DMA((HALVES,)),
            pltpu.SemaphoreType.DMA((9,)),
            pltpu.SemaphoreType.DMA((ROUNDS, HALVES, 6)),
            pltpu.SemaphoreType.DMA((ROUNDS, HALVES, 6)),
        ],
        compiler_params=pltpu.CompilerParams(collective_id=0, has_side_effects=True, vmem_limit_bytes=32 * 1024 * 1024),
    )(*(pltpu.with_memory_space_constraint(value, pltpu.HBM) for value in (
        load_raw.reshape(elements, groups, 8, nodes), fine_matrix, fine_inverse, scaling, prolong_four.T, coarse_four,
        prolong_two.T, coarse_two, orient, boundary.transpose(1, 2, 3, 0),
    )))
    return out.reshape(load_raw.shape)


def solution(mesh):
    in_specs = (
        P("ex", "ey", "ez", None, None),
        P("ex", "ey", "ez", None),
        P(),
        P(),
        P(),
        P(),
        P(),
        P(),
        P(None, "ex", "ey", "ez"),
        P(None, "ex", "ey", "ez"),
    )
    out_specs = P("ex", "ey", "ez", None, None)
    return jax.shard_map(body, mesh=mesh, in_specs=in_specs, out_specs=out_specs, check_vma=False)
```

```python
import jax
import jax.numpy as jnp
from jax import lax
from jax.experimental import pallas as pl
from jax.experimental.pallas import tpu as pltpu
from jax.sharding import PartitionSpec as P

CYCLES = 2
ROUNDS = 2 * CYCLES
HALVES = 2
AXES = ("ex", "ey", "ez")
ORDER = (1, 0, 2)

fine_weight = 0.5
coarse_weight = 0.5


def parts_of(value):
    high = value.astype(jnp.bfloat16)
    low = (value - high.astype(jnp.float32)).astype(jnp.bfloat16)
    return high, low


def small_dot(left, right):
    left_high, left_low = parts_of(left)
    right_high, right_low = parts_of(right)

    def one(a, b):
        return jnp.dot(a, b, preferred_element_type=jnp.float32)

    return one(left_high, right_high) + one(left_low, right_high) + one(left_high, right_low)


def kernel(
    load_hbm, fine_matrix_hbm, fine_inverse_hbm, scaling_hbm, prolong_four_hbm, coarse_four_hbm, prolong_two_hbm,
    coarse_two_hbm, orient_hbm, boundary_hbm,
    out_ref,
    load_v, y_v, local_v, assembled_v, first_v, matrix_v, operator_v, smoother_v,
    scaling_ref, prolong_four_ref, coarse_four_ref, prolong_two_ref, coarse_two_ref, orient_ref, boundary_ref,
    index_v, face_index_v, keep_inverse_v, inverse_v, keep_scale_v, scale_v, keep_v,
    sent_xy, sent_z, got_xy, got_z,
    load_sem, small_sem, send_sem, recv_sem,
):
    groups = load_v.shape[1] // HALVES
    position = [lax.axis_index(axis) for axis in AXES]
    size = [lax.axis_size(axis) for axis in AXES]
    has_below = [position[a] > 0 for a in range(3)]
    has_above = [position[a] < size[a] - 1 for a in range(3)]

    def load_copy(half):
        rows = pl.ds(half * groups, groups)
        return pltpu.make_async_copy(load_hbm.at[:, rows], load_v.at[:, rows], load_sem.at[half])

    barrier = pltpu.get_barrier_semaphore()
    for a in range(3):
        for there, step in ((has_below[a], -1), (has_above[a], 1)):

            @pl.when(there)
            def _():
                pl.semaphore_signal(
                    barrier, inc=1, device_id={AXES[a]: position[a] + step}, device_id_type=pl.DeviceIdType.MESH
                )

    small = [
        pltpu.make_async_copy(source, target, small_sem.at[n])
        for n, (source, target) in enumerate(
            (
                (orient_hbm, orient_ref),
                (boundary_hbm, boundary_ref),
                (scaling_hbm, scaling_ref),
                (coarse_four_hbm, coarse_four_ref),
                (prolong_four_hbm, prolong_four_ref),
                (coarse_two_hbm, coarse_two_ref),
                (prolong_two_hbm, prolong_two_ref),
                (fine_inverse_hbm, matrix_v.at[0]),
                (fine_matrix_hbm, matrix_v.at[1]),
            )
        )
    ]
    small[0].start()
    for half in range(HALVES):
        load_copy(half).start()
    lane = lax.broadcasted_iota(jnp.int32, (8, 128), 1)
    lower_half = lane < 64

    small[0].wait()

    def mask_of(a, i, j, k):
        code = orient_ref[a, i, j, k]
        return (code & 1) * 56 + (code >> 1) * 7

    for i in range(2):
        for j in range(2):
            for k in range(4):
                e = (i * 2 + j) * 4 + k
                for a in range(3):
                    above = [i, j, k]
                    above[a] += 1
                    own = mask_of(a, i, j, k)
                    if above[a] < (2, 2, 4)[a]:
                        bits = jnp.where(lower_half, mask_of(a, *above), own)
                    else:
                        bits = jnp.full((8, 128), own, jnp.int32)
                    index_v[a, e] = (lane ^ 64) ^ bits
                    if (i, j, k)[a] == 0:
                        parity = j if a == 2 else k % 2
                        slot = (j * 4 + k, i * 4 + k, i * 2 + j)[a]
                        face_index_v[a, slot] = lane ^ (own ^ (64 * parity))

    def clear(turns):
        for a in range(3):
            for there, direction in ((has_above[a], 0), (has_below[a], 1)):

                @pl.when(jnp.logical_not(there))
                def _():
                    for turn in turns:
                        for half in range(HALVES):
                            if a < 2:
                                got_xy[turn, half, 2 * a + direction] = jnp.zeros(got_xy.shape[3:], jnp.float32)
                            else:
                                got_z[turn, half, direction] = jnp.zeros(got_z.shape[3:], jnp.float32)

    def face_copy(turn, half, a, direction):
        channel = 2 * a + direction
        if a < 2:
            source, target = sent_xy.at[turn, half, channel], got_xy.at[turn, half, channel]
        else:
            source, target = sent_z.at[turn, half, direction], got_z.at[turn, half, direction]
        return pltpu.make_async_remote_copy(
            source, target, send_sem.at[half, channel], recv_sem.at[turn % 2, half, channel],
            device_id={AXES[a]: position[a] + (1 if direction else -1)}, device_id_type=pl.DeviceIdType.MESH,
        )

    def rolled(value):
        return pltpu.roll(value.reshape(-1, 128), 64, 1).reshape(value.shape)

    def gathered(value, index):
        index = jnp.broadcast_to(index, value.shape)
        return lax.gather(
            value.reshape(-1, 128),
            index.reshape(-1, 128, 1),
            lax.GatherDimensionNumbers(
                offset_dims=(), collapsed_slice_dims=(1,), start_index_map=(1,),
                operand_batching_dims=(0,), start_indices_batching_dims=(0,),
            ),
            slice_sizes=(1, 1),
            mode=lax.GatherScatterMode.PROMISE_IN_BOUNDS,
        ).reshape(value.shape)

    def edge(value, a, last):
        layer = lax.index_in_dim(value, -1 if last else 0, a, keepdims=False)
        if a < 2:
            layer = layer.reshape((2, 2, 2) + layer.shape[2:])
            return layer[:, :, 0], layer[:, :, 1]
        return layer[:, 0], layer[:, 1]

    def shaped(value):
        return value.reshape((2, 2, 4) + value.shape[1:])

    def face_index(a, parity):
        lead = (2,) if a == 2 else (2, 2)
        index = face_index_v[a, : 4 if a == 2 else 8].reshape(lead + (2, 8, 128))
        return lax.index_in_dim(index, parity, len(lead), keepdims=True)

    def pack(turn, half, source, a):
        source = shaped(source)
        first, second = edge(source, a, False)
        down = jnp.where(lower_half, gathered(first, face_index(a, 0)), gathered(second, face_index(a, 1)))
        first, second = edge(source, a, True)
        up = jnp.where(lower_half, rolled(first), second)
        if a < 2:
            sent_xy[turn, half, 2 * a] = down.reshape(sent_xy.shape[3:])
            sent_xy[turn, half, 2 * a + 1] = up.reshape(sent_xy.shape[3:])
        else:
            sent_z[turn, half, 0] = down.reshape(sent_z.shape[3:])
            sent_z[turn, half, 1] = up.reshape(sent_z.shape[3:])

    def prepare(half, source_of, base_ref, sign):
        for a in range(3):
            source = source_of(a)
            swapped = shaped(gathered(source, index_v[a][:, None]))
            count = swapped.shape[a]
            zero = jnp.zeros_like(lax.slice_in_dim(swapped, 0, 1, axis=a))
            from_below = jnp.concatenate([zero, lax.slice_in_dim(swapped, 0, count - 1, axis=a)], a)
            from_above = jnp.concatenate([lax.slice_in_dim(swapped, 1, count, axis=a), zero], a)
            total = source + jnp.where(lower_half, from_below, from_above).reshape(source.shape)
            if base_ref is not None:
                total = base_ref[half, a] + sign * total
            local_v[half, a] = total

    def send(turn, half, a):
        for there, direction in ((has_below[a], 0), (has_above[a], 1)):

            @pl.when(there)
            def _():
                face_copy(turn, half, a, direction).start()

    def sent(turn, half):
        for a in ORDER:
            for there, direction in ((has_below[a], 0), (has_above[a], 1)):

                @pl.when(there)
                def _():
                    face_copy(turn, half, a, direction).wait_send()

    def receive(turn, half):
        for a in ORDER:
            for there, direction in ((has_below[a], 1), (has_above[a], 0)):

                @pl.when(there)
                def _():
                    face_copy(turn, half, a, direction).wait_recv()

    def assembled_sum(turn, half, a, sign=1):
        local = shaped(local_v[half, a])
        if a < 2:
            down, up = got_xy[turn, half, 2 * a], got_xy[turn, half, 2 * a + 1]
            lead = (2, 2)
        else:
            down, up = got_z[turn, half, 0], got_z[turn, half, 1]
            lead = (2,)
        wide = lead + down.shape[1:]
        down, up = down.reshape(wide), up.reshape(wide)
        top = jnp.stack([rolled(down), down], len(lead))
        low = jnp.stack([gathered(up, face_index(a, parity)) for parity in range(2)], len(lead))
        layer = list(local.shape)
        layer[a] = 1
        low = jnp.where(lower_half, low, 0.0).reshape(layer)
        top = jnp.where(lower_half, 0.0, top).reshape(layer)
        count = local.shape[a]
        pieces = [
            lax.slice_in_dim(local, 0, 1, axis=a) + sign * low,
            lax.slice_in_dim(local, count - 1, count, axis=a) + sign * top,
        ]
        if count > 2:
            pieces.insert(1, lax.slice_in_dim(local, 1, count - 1, axis=a))
        return jnp.concatenate(pieces, a).reshape((16,) + local.shape[3:])

    def columns(a):
        return slice(a * 128, (a + 1) * 128)

    def multiply_and_send(turn, half, row_parts, matrix_ref, factor_ref):
        rows = jnp.concatenate([part for parts in row_parts for part in parts], -1)
        for a in ORDER:
            blocks = [rows] if a != ORDER[-1] else [rows[: rows.shape[0] // 2], rows[rows.shape[0] // 2 :]]
            outs = [jnp.dot(block, matrix_ref[a], preferred_element_type=jnp.float32) for block in blocks]
            out = jnp.concatenate([out[:, :128] + out[:, 128:] for out in outs], 0)
            piece = out.reshape(16, groups, 8, 128) * factor_ref[:, :, columns(a)][:, None]
            y_v[half, a] = piece
            pack(turn, half, piece, a)
        for a in ORDER:
            send(turn, half, a)

    def set_matrix(value, matrix_ref):
        high, low = parts_of(value)
        for a in range(3):
            for b in range(3):
                block = jnp.concatenate(
                    [part[b * 128 : (b + 1) * 128, a * 128 : (a + 1) * 128] for part in (high, low)], -1
                )
                matrix_ref[a, 2 * b * 128 : (2 * b + 1) * 128] = block
                matrix_ref[a, (2 * b + 1) * 128 : (2 * b + 2) * 128] = block

    def half_rows(ref, half, a):
        return ref[:, half * groups : (half + 1) * groups, :, columns(a)]

    pl.semaphore_wait(barrier, sum(there.astype(jnp.int32) for there in has_below + has_above))

    for half in range(HALVES):
        load_copy(half).wait()
        if half == 0:
            for copy in small[1:]:
                copy.start()
        for a in ORDER:
            pack(0, half, half_rows(load_v, half, a), a)
        for a in ORDER:
            send(0, half, a)

    clear(range(1))
    small[1].wait()
    small[2].wait()
    for i in range(2):
        for j in range(2):
            for k in range(4):
                e = (i * 2 + j) * 4 + k
                row = jnp.broadcast_to(scaling_ref[i, j, k : k + 1, :], (8, scaling_ref.shape[-1]))
                inverse = 1.0 / row
                keeps = []
                for a in range(3):
                    low_zero = jnp.where((i, j, k)[a] == 0, jnp.where(position[a] == 0, boundary_ref[i, j, k, 2 * a], 0), 0)
                    at_top = (i, j, k)[a] == (2, 2, 4)[a] - 1
                    top_zero = jnp.where(at_top, jnp.where(position[a] == size[a] - 1, boundary_ref[i, j, k, 2 * a + 1], 0), 0)
                    keeps.append((1 - jnp.where(lower_half, low_zero, top_zero)).astype(jnp.float32))
                keep = jnp.concatenate(keeps, -1)
                scale_v[e] = row
                inverse_v[e] = inverse
                keep_scale_v[e] = keep * row
                keep_inverse_v[e] = keep * inverse
                keep_v[e] = keep

    for copy in small[3:8]:
        copy.wait()
    coarse = small_dot(
        prolong_four_ref[...].T, small_dot(coarse_four_ref[...], prolong_four_ref[...])
    ) + small_dot(prolong_two_ref[...].T, small_dot(coarse_two_ref[...], prolong_two_ref[...]))
    set_matrix(fine_weight * matrix_v[0] + coarse_weight * coarse, smoother_v)

    def flat_parts(value):
        return parts_of(value.reshape(-1, 128))

    def made(half):
        return lambda a: y_v[half, a]

    for half in range(HALVES):
        prepare(half, lambda a, half=half: half_rows(load_v, half, a), None, 1)
    for half in range(HALVES):
        sent(0, half)
    for half in range(HALVES):
        receive(0, half)
        row_parts = []
        for a in range(3):
            total = assembled_sum(0, half, a)
            assembled_v[half, a] = total
            row_parts.append(flat_parts(total * keep_inverse_v[:, :, columns(a)][:, None]))
        multiply_and_send(1, half, row_parts, smoother_v, inverse_v)
    clear(range(1, ROUNDS))
    small[8].wait()
    set_matrix(matrix_v[1], operator_v)
    for half in range(HALVES):
        prepare(half, made(half), None, 1)
    for half in range(HALVES):
        sent(1, half)
    for half in range(HALVES):
        receive(1, half)
        row_parts = []
        for a in range(3):
            total = assembled_sum(1, half, a)
            first_v[half, a] = total
            row_parts.append(flat_parts(total * keep_scale_v[:, :, columns(a)][:, None]))
        multiply_and_send(2, half, row_parts, operator_v, scale_v)
    for half in range(HALVES):
        prepare(half, made(half), assembled_v, -1)
    for half in range(HALVES):
        sent(2, half)
    for half in range(HALVES):
        receive(2, half)
        row_parts = []
        for a in range(3):
            total = assembled_sum(2, half, a, -1)
            row_parts.append(flat_parts(total * keep_inverse_v[:, :, columns(a)][:, None]))
        multiply_and_send(3, half, row_parts, smoother_v, inverse_v)
    for half in range(HALVES):
        prepare(half, made(half), first_v, 1)
    for half in range(HALVES):
        sent(3, half)
    for half in range(HALVES):
        receive(3, half)
        for a in range(3):
            total = assembled_sum(3, half, a)
            out_ref[:, half * groups : (half + 1) * groups, :, columns(a)] = total * keep_v[:, :, columns(a)][:, None]


def body(
    load_raw, scaling, fine_matrix, fine_inverse, prolong_four, coarse_four, prolong_two, coarse_two, orient, boundary
):
    nodes = load_raw.shape[-1]
    groups = load_raw.shape[3] // 8
    local = groups // HALVES
    elements = 16
    f32, bf16 = jnp.float32, jnp.bfloat16
    per_half = pltpu.VMEM((HALVES, 3, elements, local, 8, 128), f32)
    factor = pltpu.VMEM((elements, 8, nodes), f32)
    out = pl.pallas_call(
        kernel,
        out_shape=pltpu.VMEM((elements, groups, 8, nodes), f32),
        in_specs=[pl.BlockSpec(memory_space=pltpu.HBM)] * 10,
        out_specs=pl.BlockSpec(memory_space=pltpu.VMEM),
        scratch_shapes=[
            pltpu.VMEM((elements, groups, 8, nodes), f32),
            per_half, per_half, per_half, per_half,
            pltpu.VMEM((2, nodes, nodes), f32),
            pltpu.VMEM((3, 2 * nodes, 256), bf16),
            pltpu.VMEM((3, 2 * nodes, 256), bf16),
            pltpu.VMEM(scaling.shape, f32),
            pltpu.VMEM(prolong_four.shape[::-1], f32),
            pltpu.VMEM(coarse_four.shape, f32),
            pltpu.VMEM(prolong_two.shape[::-1], f32),
            pltpu.VMEM(coarse_two.shape, f32),
            pltpu.SMEM(orient.shape, jnp.int32),
            pltpu.SMEM(boundary.shape[1:] + boundary.shape[:1], jnp.int32),
            pltpu.VMEM((3, elements, 8, 128), jnp.int32),
            pltpu.VMEM((3, 8, 8, 128), jnp.int32),
            factor, factor, factor, factor, factor,
            pltpu.VMEM((ROUNDS, HALVES, 4, 4, local, 8, 128), f32),
            pltpu.VMEM((ROUNDS, HALVES, 2, 2, local, 8, 128), f32),
            pltpu.VMEM((ROUNDS, HALVES, 4, 4, local, 8, 128), f32),
            pltpu.VMEM((ROUNDS, HALVES, 2, 2, local, 8, 128), f32),
            pltpu.SemaphoreType.DMA((HALVES,)),
            pltpu.SemaphoreType.DMA((9,)),
            pltpu.SemaphoreType.DMA((HALVES, 6)),
            pltpu.SemaphoreType.DMA((2, HALVES, 6)),
        ],
        compiler_params=pltpu.CompilerParams(collective_id=0, has_side_effects=True, vmem_limit_bytes=32 * 1024 * 1024),
    )(*(pltpu.with_memory_space_constraint(value, pltpu.HBM) for value in (
        load_raw.reshape(elements, groups, 8, nodes), fine_matrix, fine_inverse, scaling, prolong_four.T, coarse_four,
        prolong_two.T, coarse_two, orient, boundary.transpose(1, 2, 3, 0),
    )))
    return out.reshape(load_raw.shape)


def solution(mesh):
    in_specs = (
        P("ex", "ey", "ez", None, None),
        P("ex", "ey", "ez", None),
        P(),
        P(),
        P(),
        P(),
        P(),
        P(),
        P(None, "ex", "ey", "ez"),
        P(None, "ex", "ey", "ez"),
    )
    out_specs = P("ex", "ey", "ez", None, None)
    return jax.shard_map(body, mesh=mesh, in_specs=in_specs, out_specs=out_specs, check_vma=False)
```

```python
import jax
import jax.numpy as jnp
from jax import lax
from jax.experimental import pallas as pl
from jax.experimental.pallas import tpu as pltpu
from jax.sharding import PartitionSpec as P

CYCLES = 2
ROUNDS = 2 * CYCLES
HALVES = 2
AXES = ("ex", "ey", "ez")
LOCAL = (2, 2, 4)
ELEMENTS = [(i, j, k) for i in range(2) for j in range(2) for k in range(4)]
ORDER = (1, 0, 2)

fine_weight = 0.5
coarse_weight = 0.5


def parts_of(value):
    high = value.astype(jnp.bfloat16)
    low = (value - high.astype(jnp.float32)).astype(jnp.bfloat16)
    return high, low


def small_dot(left, right):
    left_high, left_low = parts_of(left)
    right_high, right_low = parts_of(right)

    def one(a, b):
        return jnp.dot(a, b, preferred_element_type=jnp.float32)

    return one(left_high, right_high) + one(left_low, right_high) + one(left_high, right_low)


def steps(
    load_hbm, fine_matrix_hbm, fine_inverse_hbm, scaling_hbm, prolong_four_hbm, coarse_four_hbm, prolong_two_hbm,
    coarse_two_hbm, orient_hbm, boundary_hbm,
    out_ref,
    load_v, y_v, local_v, assembled_v, first_v, matrix_v, operator_v, smoother_v,
    scaling_ref, prolong_four_ref, coarse_four_ref, prolong_two_ref, coarse_two_ref, orient_ref, boundary_ref,
    index_v, face_index_v, keep_inverse_v, inverse_v, keep_scale_v, scale_v, keep_v,
    sent_xy, sent_z, got_xy, got_z,
    load_sem, small_sem, send_sem, recv_sem,
):
    groups = load_v.shape[1] // HALVES
    position = [lax.axis_index(axis) for axis in AXES]
    size = [lax.axis_size(axis) for axis in AXES]
    has_below = [position[a] > 0 for a in range(3)]
    has_above = [position[a] < size[a] - 1 for a in range(3)]

    def load_copy(half):
        rows = pl.ds(half * groups, groups)
        return pltpu.make_async_copy(load_hbm.at[:, rows], load_v.at[:, rows], load_sem.at[half])

    barrier = pltpu.get_barrier_semaphore()
    for a in range(3):
        for there, step in ((has_below[a], -1), (has_above[a], 1)):

            @pl.when(there)
            def _():
                pl.semaphore_signal(
                    barrier, inc=1, device_id={AXES[a]: position[a] + step}, device_id_type=pl.DeviceIdType.MESH
                )

    small = [
        pltpu.make_async_copy(source, target, small_sem.at[n])
        for n, (source, target) in enumerate(
            (
                (orient_hbm, orient_ref),
                (boundary_hbm, boundary_ref),
                (scaling_hbm, scaling_ref),
                (coarse_four_hbm, coarse_four_ref),
                (prolong_four_hbm, prolong_four_ref),
                (coarse_two_hbm, coarse_two_ref),
                (prolong_two_hbm, prolong_two_ref),
                (fine_inverse_hbm, matrix_v.at[0]),
            )
        )
    ]
    small.append(pltpu.make_async_copy(fine_matrix_hbm, matrix_v.at[1], small_sem.at[0]))
    small[0].start()
    for half in range(HALVES):
        load_copy(half).start()
    lane = lax.broadcasted_iota(jnp.int32, (8, 128), 1)
    lower_half = lane < 64

    small[0].wait()

    def mask_of(a, i, j, k):
        code = orient_ref[a, i, j, k]
        return (code & 1) * 56 + (code >> 1) * 7

    for a in range(3):
        for i, j, k in ELEMENTS:
            if (i, j, k)[a] == 0:
                parity = j if a == 2 else k % 2
                slot = (j * 4 + k, i * 4 + k, i * 2 + j)[a]
                face_index_v[a, slot] = lane ^ (mask_of(a, i, j, k) ^ (64 * parity))

    def set_indices():
        for e, element in enumerate(ELEMENTS):
            for a in range(3):
                above = list(element)
                above[a] += 1
                own = mask_of(a, *element)
                if above[a] < LOCAL[a]:
                    bits = jnp.where(lower_half, mask_of(a, *above), own)
                else:
                    bits = jnp.full((8, 128), own, jnp.int32)
                index_v[a, e] = (lane ^ 64) ^ bits

    def clear(turns):
        for a in range(3):
            for there, direction in ((has_above[a], 0), (has_below[a], 1)):

                @pl.when(jnp.logical_not(there))
                def _():
                    for turn in turns:
                        for half in range(HALVES):
                            if a < 2:
                                got_xy[turn, half, 2 * a + direction] = jnp.zeros(got_xy.shape[3:], jnp.float32)
                            else:
                                got_z[turn, half, direction] = jnp.zeros(got_z.shape[3:], jnp.float32)

    def face_copy(turn, half, a, direction):
        channel = 2 * a + direction
        if a < 2:
            source, target = sent_xy.at[turn, half, channel], got_xy.at[turn, half, channel]
        else:
            source, target = sent_z.at[turn, half, direction], got_z.at[turn, half, direction]
        return pltpu.make_async_remote_copy(
            source, target, send_sem.at[half, channel], recv_sem.at[turn % 2, half, channel],
            device_id={AXES[a]: position[a] + (1 if direction else -1)}, device_id_type=pl.DeviceIdType.MESH,
        )

    def rolled(value):
        return pltpu.roll(value.reshape(-1, 128), 64, 1).reshape(value.shape)

    def gathered(value, index):
        index = jnp.broadcast_to(index, value.shape)
        return lax.gather(
            value.reshape(-1, 128),
            index.reshape(-1, 128, 1),
            lax.GatherDimensionNumbers(
                offset_dims=(), collapsed_slice_dims=(1,), start_index_map=(1,),
                operand_batching_dims=(0,), start_indices_batching_dims=(0,),
            ),
            slice_sizes=(1, 1),
            mode=lax.GatherScatterMode.PROMISE_IN_BOUNDS,
        ).reshape(value.shape)

    def edge(value, a, last):
        layer = lax.index_in_dim(value, -1 if last else 0, a, keepdims=False)
        if a < 2:
            layer = layer.reshape((2, 2, 2) + layer.shape[2:])
            return layer[:, :, 0], layer[:, :, 1]
        return layer[:, 0], layer[:, 1]

    def shaped(value):
        return value.reshape((2, 2, 4) + value.shape[1:])

    def face_index(a, parity):
        lead = (2,) if a == 2 else (2, 2)
        index = face_index_v[a, : 4 if a == 2 else 8].reshape(lead + (2, 8, 128))
        return lax.index_in_dim(index, parity, len(lead), keepdims=True)

    def pack(turn, half, source, a):
        source = shaped(source)
        first, second = edge(source, a, False)
        down = jnp.where(lower_half, gathered(first, face_index(a, 0)), gathered(second, face_index(a, 1)))
        first, second = edge(source, a, True)
        up = jnp.where(lower_half, rolled(first), second)
        if a < 2:
            sent_xy[turn, half, 2 * a] = down.reshape(sent_xy.shape[3:])
            sent_xy[turn, half, 2 * a + 1] = up.reshape(sent_xy.shape[3:])
        else:
            sent_z[turn, half, 0] = down.reshape(sent_z.shape[3:])
            sent_z[turn, half, 1] = up.reshape(sent_z.shape[3:])

    def prepare(half, source_of, base_ref, sign):
        for a in range(3):
            source = source_of(a)
            swapped = shaped(gathered(source, index_v[a][:, None]))
            count = swapped.shape[a]
            zero = jnp.zeros_like(lax.slice_in_dim(swapped, 0, 1, axis=a))
            from_below = jnp.concatenate([zero, lax.slice_in_dim(swapped, 0, count - 1, axis=a)], a)
            from_above = jnp.concatenate([lax.slice_in_dim(swapped, 1, count, axis=a), zero], a)
            total = source + jnp.where(lower_half, from_below, from_above).reshape(source.shape)
            if base_ref is not None:
                total = base_ref[half, a] + sign * total
            local_v[half, a] = total

    def send(turn, half, a):
        for there, direction in ((has_below[a], 0), (has_above[a], 1)):

            @pl.when(there)
            def _():
                face_copy(turn, half, a, direction).start()

    def sent(turn, half):
        for a in ORDER:
            for there, direction in ((has_below[a], 0), (has_above[a], 1)):

                @pl.when(there)
                def _():
                    face_copy(turn, half, a, direction).wait_send()

    def receive(turn, half):
        for a in ORDER:
            for there, direction in ((has_below[a], 1), (has_above[a], 0)):

                @pl.when(there)
                def _():
                    face_copy(turn, half, a, direction).wait_recv()

    def assembled_sum(turn, half, a, sign=1):
        local = shaped(local_v[half, a])
        if a < 2:
            down, up = got_xy[turn, half, 2 * a], got_xy[turn, half, 2 * a + 1]
            lead = (2, 2)
        else:
            down, up = got_z[turn, half, 0], got_z[turn, half, 1]
            lead = (2,)
        wide = lead + down.shape[1:]
        down, up = down.reshape(wide), up.reshape(wide)
        top = jnp.stack([rolled(down), down], len(lead))
        low = jnp.stack([gathered(up, face_index(a, parity)) for parity in range(2)], len(lead))
        layer = list(local.shape)
        layer[a] = 1
        low = jnp.where(lower_half, low, 0.0).reshape(layer)
        top = jnp.where(lower_half, 0.0, top).reshape(layer)
        count = local.shape[a]
        pieces = [
            lax.slice_in_dim(local, 0, 1, axis=a) + sign * low,
            lax.slice_in_dim(local, count - 1, count, axis=a) + sign * top,
        ]
        if count > 2:
            pieces.insert(1, lax.slice_in_dim(local, 1, count - 1, axis=a))
        return jnp.concatenate(pieces, a).reshape((16,) + local.shape[3:])

    def columns(a):
        return slice(a * 128, (a + 1) * 128)

    def multiply_and_send(turn, half, row_parts, matrix_ref, factor_ref):
        rows = jnp.concatenate([part for parts in row_parts for part in parts], -1)
        for a in ORDER:
            blocks = [rows] if a != ORDER[-1] else [rows[: rows.shape[0] // 2], rows[rows.shape[0] // 2 :]]
            outs = [jnp.dot(block, matrix_ref[a], preferred_element_type=jnp.float32) for block in blocks]
            out = jnp.concatenate([out[:, :128] + out[:, 128:] for out in outs], 0)
            piece = out.reshape(16, groups, 8, 128) * factor_ref[:, :, columns(a)][:, None]
            y_v[half, a] = piece
            pack(turn, half, piece, a)
        for a in ORDER:
            send(turn, half, a)

    def set_matrix(value, matrix_ref):
        high, low = parts_of(value)
        for a in range(3):
            for b in range(3):
                block = jnp.concatenate(
                    [part[b * 128 : (b + 1) * 128, a * 128 : (a + 1) * 128] for part in (high, low)], -1
                )
                matrix_ref[a, 2 * b * 128 : (2 * b + 1) * 128] = block
                matrix_ref[a, (2 * b + 1) * 128 : (2 * b + 2) * 128] = block

    def half_rows(ref, half, a):
        return ref[:, half * groups : (half + 1) * groups, :, columns(a)]

    for half in range(HALVES):
        load_copy(half).wait()
        if half == 0:
            for copy in small[1:]:
                copy.start()
        for a in ORDER:
            pack(0, half, half_rows(load_v, half, a), a)
        if half == 0:
            pl.semaphore_wait(barrier, sum(there.astype(jnp.int32) for there in has_below + has_above))
        for a in ORDER:
            send(0, half, a)

    set_indices()
    clear(range(1))
    small[1].wait()
    small[2].wait()
    for i in range(2):
        for j in range(2):
            for k in range(4):
                e = (i * 2 + j) * 4 + k
                row = jnp.broadcast_to(scaling_ref[i, j, k : k + 1, :], (8, scaling_ref.shape[-1]))
                inverse = 1.0 / row
                keeps = []
                for a in range(3):
                    low_zero = jnp.where((i, j, k)[a] == 0, jnp.where(position[a] == 0, boundary_ref[i, j, k, 2 * a], 0), 0)
                    at_top = (i, j, k)[a] == (2, 2, 4)[a] - 1
                    top_zero = jnp.where(at_top, jnp.where(position[a] == size[a] - 1, boundary_ref[i, j, k, 2 * a + 1], 0), 0)
                    keeps.append((1 - jnp.where(lower_half, low_zero, top_zero)).astype(jnp.float32))
                keep = jnp.concatenate(keeps, -1)
                scale_v[e] = row
                inverse_v[e] = inverse
                keep_scale_v[e] = keep * row
                keep_inverse_v[e] = keep * inverse
                keep_v[e] = keep

    for copy in small[3:8]:
        copy.wait()
    coarse = small_dot(
        prolong_four_ref[...].T, small_dot(coarse_four_ref[...], prolong_four_ref[...])
    ) + small_dot(prolong_two_ref[...].T, small_dot(coarse_two_ref[...], prolong_two_ref[...]))
    set_matrix(fine_weight * matrix_v[0] + coarse_weight * coarse, smoother_v)

    def flat_parts(value):
        return parts_of(value.reshape(-1, 128))

    def made(half):
        return lambda a: y_v[half, a]

    for half in range(HALVES):
        prepare(half, lambda a, half=half: half_rows(load_v, half, a), None, 1)
    for half in range(HALVES):
        sent(0, half)
    for half in range(HALVES):
        receive(0, half)
        row_parts = []
        for a in range(3):
            total = assembled_sum(0, half, a)
            assembled_v[half, a] = total
            row_parts.append(flat_parts(total * keep_inverse_v[:, :, columns(a)][:, None]))
        multiply_and_send(1, half, row_parts, smoother_v, inverse_v)
    clear(range(1, ROUNDS))
    small[8].wait()
    set_matrix(matrix_v[1], operator_v)
    for half in range(HALVES):
        prepare(half, made(half), None, 1)
    for half in range(HALVES):
        sent(1, half)
    for half in range(HALVES):
        receive(1, half)
        row_parts = []
        for a in range(3):
            total = assembled_sum(1, half, a)
            first_v[half, a] = total
            row_parts.append(flat_parts(total * keep_scale_v[:, :, columns(a)][:, None]))
        multiply_and_send(2, half, row_parts, operator_v, scale_v)
    for half in range(HALVES):
        prepare(half, made(half), assembled_v, -1)
    for half in range(HALVES):
        sent(2, half)
    for half in range(HALVES):
        receive(2, half)
        row_parts = []
        for a in range(3):
            total = assembled_sum(2, half, a, -1)
            row_parts.append(flat_parts(total * keep_inverse_v[:, :, columns(a)][:, None]))
        multiply_and_send(3, half, row_parts, smoother_v, inverse_v)
    for half in range(HALVES):
        prepare(half, made(half), first_v, 1)
    for half in range(HALVES):
        sent(3, half)
    for half in range(HALVES):
        receive(3, half)
        for a in range(3):
            total = assembled_sum(3, half, a)
            out_ref[:, half * groups : (half + 1) * groups, :, columns(a)] = total * keep_v[:, :, columns(a)][:, None]


def kernel(*refs):
    pl.run_scoped(
        lambda load_sem, small_sem, send_sem: steps(*refs[:-1], load_sem, small_sem, send_sem, refs[-1]),
        pltpu.SemaphoreType.DMA((HALVES,)),
        pltpu.SemaphoreType.DMA((8,)),
        pltpu.SemaphoreType.DMA((HALVES, 6)),
    )


def body(
    load_raw, scaling, fine_matrix, fine_inverse, prolong_four, coarse_four, prolong_two, coarse_two, orient, boundary
):
    nodes = load_raw.shape[-1]
    groups = load_raw.shape[3] // 8
    local = groups // HALVES
    elements = 16
    f32, bf16 = jnp.float32, jnp.bfloat16
    per_half = pltpu.VMEM((HALVES, 3, elements, local, 8, 128), f32)
    factor = pltpu.VMEM((elements, 8, nodes), f32)
    out = pl.pallas_call(
        kernel,
        out_shape=pltpu.VMEM((elements, groups, 8, nodes), f32),
        in_specs=[pl.BlockSpec(memory_space=pltpu.HBM)] * 10,
        out_specs=pl.BlockSpec(memory_space=pltpu.VMEM),
        scratch_shapes=[
            pltpu.VMEM((elements, groups, 8, nodes), f32),
            per_half, per_half, per_half, per_half,
            pltpu.VMEM((2, nodes, nodes), f32),
            pltpu.VMEM((3, 2 * nodes, 256), bf16),
            pltpu.VMEM((3, 2 * nodes, 256), bf16),
            pltpu.VMEM(scaling.shape, f32),
            pltpu.VMEM(prolong_four.shape[::-1], f32),
            pltpu.VMEM(coarse_four.shape, f32),
            pltpu.VMEM(prolong_two.shape[::-1], f32),
            pltpu.VMEM(coarse_two.shape, f32),
            pltpu.SMEM(orient.shape, jnp.int32),
            pltpu.SMEM(boundary.shape[1:] + boundary.shape[:1], jnp.int32),
            pltpu.VMEM((3, elements, 8, 128), jnp.int32),
            pltpu.VMEM((3, 8, 8, 128), jnp.int32),
            factor, factor, factor, factor, factor,
            pltpu.VMEM((ROUNDS, HALVES, 4, 4, local, 8, 128), f32),
            pltpu.VMEM((ROUNDS, HALVES, 2, 2, local, 8, 128), f32),
            pltpu.VMEM((ROUNDS, HALVES, 4, 4, local, 8, 128), f32),
            pltpu.VMEM((ROUNDS, HALVES, 2, 2, local, 8, 128), f32),
            pltpu.SemaphoreType.DMA((2, HALVES, 6)),
        ],
        compiler_params=pltpu.CompilerParams(collective_id=0, has_side_effects=True, vmem_limit_bytes=32 * 1024 * 1024),
    )(*(pltpu.with_memory_space_constraint(value, pltpu.HBM) for value in (
        load_raw.reshape(elements, groups, 8, nodes), fine_matrix, fine_inverse, scaling, prolong_four.T, coarse_four,
        prolong_two.T, coarse_two, orient, boundary.transpose(1, 2, 3, 0),
    )))
    return out.reshape(load_raw.shape)


def solution(mesh):
    in_specs = (
        P("ex", "ey", "ez", None, None),
        P("ex", "ey", "ez", None),
        P(),
        P(),
        P(),
        P(),
        P(),
        P(),
        P(None, "ex", "ey", "ez"),
        P(None, "ex", "ey", "ez"),
    )
    out_specs = P("ex", "ey", "ez", None, None)
    return jax.shard_map(body, mesh=mesh, in_specs=in_specs, out_specs=out_specs, check_vma=False)
```

```python
import jax
import jax.numpy as jnp
from jax import lax
from jax.experimental import pallas as pl
from jax.experimental.pallas import tpu as pltpu
from jax.sharding import PartitionSpec as P

CYCLES = 2
ROUNDS = 2 * CYCLES
HALVES = 2
AXES = ("ex", "ey", "ez")
LOCAL = (2, 2, 4)
ELEMENTS = [(i, j, k) for i in range(2) for j in range(2) for k in range(4)]
ORDER = (1, 0, 2)
DEPTH_ORDER = (2, 1, 0)

fine_weight = 0.5
coarse_weight = 0.5


def parts_of(value):
    high = value.astype(jnp.bfloat16)
    low = (value - high.astype(jnp.float32)).astype(jnp.bfloat16)
    return high, low


def small_dot(left, right):
    left_high, left_low = parts_of(left)
    right_high, right_low = parts_of(right)

    def one(a, b):
        return jnp.dot(a, b, preferred_element_type=jnp.float32)

    return one(left_high, right_high) + one(left_low, right_high) + one(left_high, right_low)


def steps(
    load_hbm, fine_matrix_hbm, fine_inverse_hbm, scaling_hbm, prolong_four_hbm, coarse_four_hbm, prolong_two_hbm,
    coarse_two_hbm, orient_hbm, boundary_hbm,
    out_ref,
    load_v, y_v, local_v, assembled_v, first_v, matrix_v, operator_v, smoother_v,
    scaling_ref, prolong_four_ref, coarse_four_ref, prolong_two_ref, coarse_two_ref, orient_ref, boundary_ref,
    index_v, face_index_v, keep_inverse_v, inverse_v, keep_scale_v, scale_v, keep_v,
    sent_xy, sent_z, got_xy, got_z,
    load_sem, small_sem, send_sem, recv_sem,
):
    groups = load_v.shape[1] // HALVES
    position = [lax.axis_index(axis) for axis in AXES]
    size = [lax.axis_size(axis) for axis in AXES]
    has_below = [position[a] > 0 for a in range(3)]
    has_above = [position[a] < size[a] - 1 for a in range(3)]

    def load_copy(half):
        rows = pl.ds(half * groups, groups)
        return pltpu.make_async_copy(load_hbm.at[:, rows], load_v.at[:, rows], load_sem.at[half])

    barrier = pltpu.get_barrier_semaphore()
    for a in range(3):
        for there, step in ((has_below[a], -1), (has_above[a], 1)):

            @pl.when(there)
            def _():
                pl.semaphore_signal(
                    barrier, inc=1, device_id={AXES[a]: position[a] + step}, device_id_type=pl.DeviceIdType.MESH
                )

    small = [
        pltpu.make_async_copy(source, target, small_sem.at[n])
        for n, (source, target) in enumerate(
            (
                (orient_hbm, orient_ref),
                (boundary_hbm, boundary_ref),
                (scaling_hbm, scaling_ref),
                (coarse_four_hbm, coarse_four_ref),
                (prolong_four_hbm, prolong_four_ref),
                (coarse_two_hbm, coarse_two_ref),
                (prolong_two_hbm, prolong_two_ref),
                (fine_inverse_hbm, matrix_v.at[0]),
            )
        )
    ]
    small.append(pltpu.make_async_copy(fine_matrix_hbm, matrix_v.at[1], small_sem.at[0]))
    small[0].start()
    for half in range(HALVES):
        load_copy(half).start()
    lane = lax.broadcasted_iota(jnp.int32, (8, 128), 1)
    lower_half = lane < 64

    small[0].wait()

    def mask_of(a, i, j, k):
        code = orient_ref[a, i, j, k]
        return (code & 1) * 56 + (code >> 1) * 7

    for a in range(3):
        for i, j, k in ELEMENTS:
            if (i, j, k)[a] == 0:
                parity = j if a == 2 else k % 2
                slot = (j * 4 + k, i * 4 + k, i * 2 + j)[a]
                face_index_v[a, slot] = lane ^ (mask_of(a, i, j, k) ^ (64 * parity))

    def set_indices():
        for e, element in enumerate(ELEMENTS):
            for a in range(3):
                above = list(element)
                above[a] += 1
                own = mask_of(a, *element)
                if above[a] < LOCAL[a]:
                    bits = jnp.where(lower_half, mask_of(a, *above), own)
                else:
                    bits = jnp.full((8, 128), own, jnp.int32)
                index_v[a, e] = (lane ^ 64) ^ bits

    def clear(turns):
        for a in range(3):
            for there, direction in ((has_above[a], 0), (has_below[a], 1)):

                @pl.when(jnp.logical_not(there))
                def _():
                    for turn in turns:
                        for half in range(HALVES):
                            if a < 2:
                                got_xy[turn, half, 2 * a + direction] = jnp.zeros(got_xy.shape[3:], jnp.float32)
                            else:
                                got_z[turn, half, direction] = jnp.zeros(got_z.shape[3:], jnp.float32)

    def face_copy(turn, half, a, direction):
        channel = 2 * a + direction
        if a < 2:
            source, target = sent_xy.at[turn, half, channel], got_xy.at[turn, half, channel]
        else:
            source, target = sent_z.at[turn, half, direction], got_z.at[turn, half, direction]
        return pltpu.make_async_remote_copy(
            source, target, send_sem.at[half, channel], recv_sem.at[turn % 2, half, channel],
            device_id={AXES[a]: position[a] + (1 if direction else -1)}, device_id_type=pl.DeviceIdType.MESH,
        )

    def rolled(value):
        return pltpu.roll(value.reshape(-1, 128), 64, 1).reshape(value.shape)

    def gathered(value, index):
        index = jnp.broadcast_to(index, value.shape)
        return lax.gather(
            value.reshape(-1, 128),
            index.reshape(-1, 128, 1),
            lax.GatherDimensionNumbers(
                offset_dims=(), collapsed_slice_dims=(1,), start_index_map=(1,),
                operand_batching_dims=(0,), start_indices_batching_dims=(0,),
            ),
            slice_sizes=(1, 1),
            mode=lax.GatherScatterMode.PROMISE_IN_BOUNDS,
        ).reshape(value.shape)

    def edge(value, a, last):
        layer = lax.index_in_dim(value, -1 if last else 0, a, keepdims=False)
        if a < 2:
            layer = layer.reshape((2, 2, 2) + layer.shape[2:])
            return layer[:, :, 0], layer[:, :, 1]
        return layer[:, 0], layer[:, 1]

    def shaped(value):
        return value.reshape((2, 2, 4) + value.shape[1:])

    def face_index(a, parity):
        lead = (2,) if a == 2 else (2, 2)
        index = face_index_v[a, : 4 if a == 2 else 8].reshape(lead + (2, 8, 128))
        return lax.index_in_dim(index, parity, len(lead), keepdims=True)

    def pack(turn, half, source, a):
        source = shaped(source)
        first, second = edge(source, a, False)
        down = jnp.where(lower_half, gathered(first, face_index(a, 0)), gathered(second, face_index(a, 1)))
        first, second = edge(source, a, True)
        up = jnp.where(lower_half, rolled(first), second)
        if a < 2:
            sent_xy[turn, half, 2 * a] = down.reshape(sent_xy.shape[3:])
            sent_xy[turn, half, 2 * a + 1] = up.reshape(sent_xy.shape[3:])
        else:
            sent_z[turn, half, 0] = down.reshape(sent_z.shape[3:])
            sent_z[turn, half, 1] = up.reshape(sent_z.shape[3:])

    def prepare(half, source_of, base_ref, sign):
        for a in range(3):
            source = source_of(a)
            swapped = shaped(gathered(source, index_v[a][:, None]))
            count = swapped.shape[a]
            zero = jnp.zeros_like(lax.slice_in_dim(swapped, 0, 1, axis=a))
            from_below = jnp.concatenate([zero, lax.slice_in_dim(swapped, 0, count - 1, axis=a)], a)
            from_above = jnp.concatenate([lax.slice_in_dim(swapped, 1, count, axis=a), zero], a)
            total = source + jnp.where(lower_half, from_below, from_above).reshape(source.shape)
            if base_ref is not None:
                total = base_ref[half, a] + sign * total
            local_v[half, a] = total

    def send(turn, half, a):
        for there, direction in ((has_below[a], 0), (has_above[a], 1)):

            @pl.when(there)
            def _():
                face_copy(turn, half, a, direction).start()

    def sent(turn, half):
        for a in ORDER:
            for there, direction in ((has_below[a], 0), (has_above[a], 1)):

                @pl.when(there)
                def _():
                    face_copy(turn, half, a, direction).wait_send()

    def receive(turn, half):
        for a in ORDER:
            for there, direction in ((has_below[a], 1), (has_above[a], 0)):

                @pl.when(there)
                def _():
                    face_copy(turn, half, a, direction).wait_recv()

    def assembled_sum(turn, half, a, sign=1):
        local = shaped(local_v[half, a])
        if a < 2:
            down, up = got_xy[turn, half, 2 * a], got_xy[turn, half, 2 * a + 1]
            lead = (2, 2)
        else:
            down, up = got_z[turn, half, 0], got_z[turn, half, 1]
            lead = (2,)
        wide = lead + down.shape[1:]
        down, up = down.reshape(wide), up.reshape(wide)
        top = jnp.stack([rolled(down), down], len(lead))
        low = jnp.stack([gathered(up, face_index(a, parity)) for parity in range(2)], len(lead))
        layer = list(local.shape)
        layer[a] = 1
        low = jnp.where(lower_half, low, 0.0).reshape(layer)
        top = jnp.where(lower_half, 0.0, top).reshape(layer)
        count = local.shape[a]
        pieces = [
            lax.slice_in_dim(local, 0, 1, axis=a) + sign * low,
            lax.slice_in_dim(local, count - 1, count, axis=a) + sign * top,
        ]
        if count > 2:
            pieces.insert(1, lax.slice_in_dim(local, 1, count - 1, axis=a))
        return jnp.concatenate(pieces, a).reshape((16,) + local.shape[3:])

    def columns(a):
        return slice(a * 128, (a + 1) * 128)

    def multiply_and_send(turn, half, row_parts, matrix_ref, factor_ref):
        rows = jnp.concatenate([part for parts in row_parts for part in parts], -1)
        for a in ORDER:
            blocks = [rows] if a != ORDER[-1] else [rows[: rows.shape[0] // 2], rows[rows.shape[0] // 2 :]]
            outs = [jnp.dot(block, matrix_ref[a], preferred_element_type=jnp.float32) for block in blocks]
            out = jnp.concatenate([out[:, :128] + out[:, 128:] for out in outs], 0)
            piece = out.reshape(16, groups, 8, 128) * factor_ref[:, :, columns(a)][:, None]
            y_v[half, a] = piece
            pack(turn, half, piece, a)
        for a in ORDER:
            send(turn, half, a)

    def set_matrix(value, matrix_ref):
        high, low = parts_of(value)
        for a in range(3):
            for at, b in enumerate(DEPTH_ORDER):
                block = jnp.concatenate(
                    [part[b * 128 : (b + 1) * 128, a * 128 : (a + 1) * 128] for part in (high, low)], -1
                )
                matrix_ref[a, 2 * at * 128 : (2 * at + 1) * 128] = block
                matrix_ref[a, (2 * at + 1) * 128 : (2 * at + 2) * 128] = block

    def half_rows(ref, half, a):
        return ref[:, half * groups : (half + 1) * groups, :, columns(a)]

    for half in range(HALVES):
        load_copy(half).wait()
        if half == 0:
            for copy in small[1:]:
                copy.start()
        for a in ORDER:
            pack(0, half, half_rows(load_v, half, a), a)
        if half == 0:
            pl.semaphore_wait(barrier, sum(there.astype(jnp.int32) for there in has_below + has_above))
        for a in ORDER:
            send(0, half, a)

    set_indices()
    clear(range(1))
    small[1].wait()
    small[2].wait()
    for i in range(2):
        for j in range(2):
            for k in range(4):
                e = (i * 2 + j) * 4 + k
                row = jnp.broadcast_to(scaling_ref[i, j, k : k + 1, :], (8, scaling_ref.shape[-1]))
                inverse = 1.0 / row
                keeps = []
                for a in range(3):
                    low_zero = jnp.where((i, j, k)[a] == 0, jnp.where(position[a] == 0, boundary_ref[i, j, k, 2 * a], 0), 0)
                    at_top = (i, j, k)[a] == (2, 2, 4)[a] - 1
                    top_zero = jnp.where(at_top, jnp.where(position[a] == size[a] - 1, boundary_ref[i, j, k, 2 * a + 1], 0), 0)
                    keeps.append((1 - jnp.where(lower_half, low_zero, top_zero)).astype(jnp.float32))
                keep = jnp.concatenate(keeps, -1)
                scale_v[e] = row
                inverse_v[e] = inverse
                keep_scale_v[e] = keep * row
                keep_inverse_v[e] = keep * inverse
                keep_v[e] = keep

    for copy in small[3:8]:
        copy.wait()
    coarse = small_dot(
        prolong_four_ref[...].T, small_dot(coarse_four_ref[...], prolong_four_ref[...])
    ) + small_dot(prolong_two_ref[...].T, small_dot(coarse_two_ref[...], prolong_two_ref[...]))
    set_matrix(fine_weight * matrix_v[0] + coarse_weight * coarse, smoother_v)

    def flat_parts(value):
        return parts_of(value.reshape(-1, 128))

    def made(half):
        return lambda a: y_v[half, a]

    for half in range(HALVES):
        prepare(half, lambda a, half=half: half_rows(load_v, half, a), None, 1)
    for half in range(HALVES):
        sent(0, half)
    for half in range(HALVES):
        receive(0, half)
        row_parts = []
        for a in DEPTH_ORDER:
            total = assembled_sum(0, half, a)
            assembled_v[half, a] = total
            row_parts.append(flat_parts(total * keep_inverse_v[:, :, columns(a)][:, None]))
        multiply_and_send(1, half, row_parts, smoother_v, inverse_v)
    clear(range(1, ROUNDS))
    small[8].wait()
    set_matrix(matrix_v[1], operator_v)
    for half in range(HALVES):
        prepare(half, made(half), None, 1)
    for half in range(HALVES):
        sent(1, half)
    for half in range(HALVES):
        receive(1, half)
        row_parts = []
        for a in DEPTH_ORDER:
            total = assembled_sum(1, half, a)
            first_v[half, a] = total
            row_parts.append(flat_parts(total * keep_scale_v[:, :, columns(a)][:, None]))
        multiply_and_send(2, half, row_parts, operator_v, scale_v)
    for half in range(HALVES):
        prepare(half, made(half), assembled_v, -1)
    for half in range(HALVES):
        sent(2, half)
    for half in range(HALVES):
        receive(2, half)
        row_parts = []
        for a in DEPTH_ORDER:
            total = assembled_sum(2, half, a, -1)
            row_parts.append(flat_parts(total * keep_inverse_v[:, :, columns(a)][:, None]))
        multiply_and_send(3, half, row_parts, smoother_v, inverse_v)
    for half in range(HALVES):
        prepare(half, made(half), first_v, 1)
    for half in range(HALVES):
        sent(3, half)
    for half in range(HALVES):
        receive(3, half)
        for a in range(3):
            total = assembled_sum(3, half, a)
            out_ref[:, half * groups : (half + 1) * groups, :, columns(a)] = total * keep_v[:, :, columns(a)][:, None]


def kernel(*refs):
    pl.run_scoped(
        lambda load_sem, small_sem, send_sem: steps(*refs[:-1], load_sem, small_sem, send_sem, refs[-1]),
        pltpu.SemaphoreType.DMA((HALVES,)),
        pltpu.SemaphoreType.DMA((8,)),
        pltpu.SemaphoreType.DMA((HALVES, 6)),
    )


def body(
    load_raw, scaling, fine_matrix, fine_inverse, prolong_four, coarse_four, prolong_two, coarse_two, orient, boundary
):
    nodes = load_raw.shape[-1]
    groups = load_raw.shape[3] // 8
    local = groups // HALVES
    elements = 16
    f32, bf16 = jnp.float32, jnp.bfloat16
    per_half = pltpu.VMEM((HALVES, 3, elements, local, 8, 128), f32)
    factor = pltpu.VMEM((elements, 8, nodes), f32)
    out = pl.pallas_call(
        kernel,
        out_shape=pltpu.VMEM((elements, groups, 8, nodes), f32),
        in_specs=[pl.BlockSpec(memory_space=pltpu.HBM)] * 10,
        out_specs=pl.BlockSpec(memory_space=pltpu.VMEM),
        scratch_shapes=[
            pltpu.VMEM((elements, groups, 8, nodes), f32),
            per_half, per_half, per_half, per_half,
            pltpu.VMEM((2, nodes, nodes), f32),
            pltpu.VMEM((3, 2 * nodes, 256), bf16),
            pltpu.VMEM((3, 2 * nodes, 256), bf16),
            pltpu.VMEM(scaling.shape, f32),
            pltpu.VMEM(prolong_four.shape[::-1], f32),
            pltpu.VMEM(coarse_four.shape, f32),
            pltpu.VMEM(prolong_two.shape[::-1], f32),
            pltpu.VMEM(coarse_two.shape, f32),
            pltpu.SMEM(orient.shape, jnp.int32),
            pltpu.SMEM(boundary.shape[1:] + boundary.shape[:1], jnp.int32),
            pltpu.VMEM((3, elements, 8, 128), jnp.int32),
            pltpu.VMEM((3, 8, 8, 128), jnp.int32),
            factor, factor, factor, factor, factor,
            pltpu.VMEM((ROUNDS, HALVES, 4, 4, local, 8, 128), f32),
            pltpu.VMEM((ROUNDS, HALVES, 2, 2, local, 8, 128), f32),
            pltpu.VMEM((ROUNDS, HALVES, 4, 4, local, 8, 128), f32),
            pltpu.VMEM((ROUNDS, HALVES, 2, 2, local, 8, 128), f32),
            pltpu.SemaphoreType.DMA((2, HALVES, 6)),
        ],
        compiler_params=pltpu.CompilerParams(collective_id=0, has_side_effects=True, vmem_limit_bytes=32 * 1024 * 1024),
    )(*(pltpu.with_memory_space_constraint(value, pltpu.HBM) for value in (
        load_raw.reshape(elements, groups, 8, nodes), fine_matrix, fine_inverse, scaling, prolong_four.T, coarse_four,
        prolong_two.T, coarse_two, orient, boundary.transpose(1, 2, 3, 0),
    )))
    return out.reshape(load_raw.shape)


def solution(mesh):
    in_specs = (
        P("ex", "ey", "ez", None, None),
        P("ex", "ey", "ez", None),
        P(),
        P(),
        P(),
        P(),
        P(),
        P(),
        P(None, "ex", "ey", "ez"),
        P(None, "ex", "ey", "ez"),
    )
    out_specs = P("ex", "ey", "ez", None, None)
    return jax.shard_map(body, mesh=mesh, in_specs=in_specs, out_specs=out_specs, check_vma=False)
```
